32 devices in a mesh: dom: 8 (over z, x), ens: 4 (over y, core).
Axes of the slice: x: 2, y: 2, z: 4, core: 2. Of those that a mesh axis runs over, the one named last changes fastest.
Arguments:
- link_flow: float32 [64, 16384], P('ens', 'dom'), may hold values from 0.2 to 1
- free_time: float32 [16384], P('dom'), may hold values from 0.1 to 4
- capacity: float32 [16384], P('dom'), may hold values from 0.5 to 1.5
- demand: float32 [64, 8, 256], P('ens', 'dom'), may hold values from 0.05 to 0.3
- path_od: int32 [8, 1024], P('dom'), may hold values from 0 to 255, never falling along the last dimension, each value on 1 to 8 neighbouring positions
- send_blocks: int32 [8, 8, 4], P('dom'), may hold values from 0 to 15
- send_counts: int32 [8, 8], P('dom'), may hold values from 0 to 4, as said below
- tile_links: int32 [8, 8, 4, 4, 128], P('dom'), may hold values from -128 to 127
- tile_paths: int32 [8, 8, 4], P('dom'), may hold values from 0 to 7
Outputs:
- link_load: float32 [64, 16384], P('ens', 'dom')
- path_flow: float32 [64, 8192], P('ens', 'dom')
- mean_time: float32 [16384], P('dom')
The draws below stay inside these ranges and needn't reach their ends.
Inputs may be any that keep to these rules, and one draw needn't show every extreme that they name: `path_od`: each row holds non-decreasing pair ids; every id of 0 .. 255 names 1 to 8 paths of its row. `send_counts`: some path owner receives 4 live tiles from every link partition.
All inputs are finite; a program needn't handle non-finite values.
Results may differ from the reference program's by a relative error of at most 0.0003.
Values sent between devices are 32-bit elements; how exact they have to be, the bound alone decides.
A program may use at most 64 MiB of HBM per device.

```python
import math
import jax
import jax.numpy as jnp
import numpy as np
from jax import lax

LINK_BLOCKS = 16
PATH_BLOCKS = 8
BLOCK = 128
CAP = 4
HOPS = 4
ITERS = 2
SCENARIOS = 64
LINKS = 16384
PATHS_DEV = 1024
OD_DEV = 256
N_DOM = 8


def draw_free_time(key, part):
    uniform_draw = jax.random.uniform(key, (LINKS,), jnp.float32)
    return jnp.exp(math.log(0.1) + uniform_draw * math.log(10.0)).astype(jnp.float32)


def draw_send_counts(key, part):
    first_key = jax.random.fold_in(key, 11)
    second_key = jax.random.fold_in(key, 23)
    baseline = jax.random.randint(first_key, (N_DOM, N_DOM), 0, CAP)
    crowded = jax.random.randint(second_key, (max(1, N_DOM // 16),), 0, N_DOM)
    crowded_mask = jnp.zeros((N_DOM,), jnp.int32).at[crowded].set(1)
    return jnp.where(crowded_mask[None, :] == 1, CAP, baseline).astype(jnp.int32)


def set_ends(entries, stream_key, low, high):
    longest = entries.shape.index(max(entries.shape))
    spots = []
    for shift in (0, 1):
        where = [jax.random.randint(jax.random.fold_in(stream_key, axis), (), 0, length) for axis, length in enumerate(entries.shape)]
        where[longest] = (where[longest] + shift) % entries.shape[longest]
        spots.append(tuple(where))
    return entries.at[spots[0]].set(low).at[spots[1]].set(high)


def block_scale(rng, extent, split, least, top_value):
    loudness = 1.0
    for position, blocks in split:
        steps = jax.random.uniform(jax.random.fold_in(jax.random.fold_in(rng, 6), position), (blocks,), jnp.float32, least / len(split), top_value / len(split))
        loudness = loudness * jnp.repeat(jnp.exp(steps), extent[position] // blocks).reshape((-1,) + (1,) * (len(extent) - 1 - position))
    return loudness


def length_profile(count, total, bound, lean):
    portions = [(1 << 20) // math.isqrt(rank ** lean) + 1 for rank in range(2, count + 1)]
    spare, given = total - bound - (count - 1), [1] * (count - 1)
    while spare > 0:
        candidates = [i for i in range(count - 1) if given[i] < bound]
        pool, remaining = sum([portions[i] for i in candidates]), spare
        for i in candidates:
            addition = min(bound - given[i], max(1, remaining * portions[i] // pool), spare)
            given[i] = given[i] + addition
            spare = spare - addition
    return np.array([bound] + given)


def ragged_sizes(stream_key, number_of, total, limit, slope):
    if number_of == 2:
        one = jax.random.randint(stream_key, (), max(1, total - limit), min(limit, total - 1) + 1)
        return jnp.stack([one, total - one])
    tallies = jnp.asarray(length_profile(number_of, total, limit, slope), jnp.int32)
    couples = (number_of - 1) // 2
    giver, sink = tallies[1:1 + 2 * couples:2], tallies[2:2 + 2 * couples:2]
    margin = jnp.minimum(giver - 1, limit - sink)
    shifted = jax.random.randint(jax.random.fold_in(stream_key, 1), (couples,), 0, 1 << 20) % (margin + 1)
    tallies = tallies.at[1:1 + 2 * couples:2].set(giver - shifted).at[2:2 + 2 * couples:2].set(sink + shifted)
    return tallies[jax.random.permutation(jax.random.fold_in(stream_key, 2), number_of)]


def setup_inputs(seed: int = 0) -> dict:
    key_of = jax.random.split(jax.random.key(seed), 10)
    link_flow = jnp.clip(jnp.exp(math.log(1.0) - 1.609438 * jax.random.uniform(key_of[0], (SCENARIOS, LINKS), jnp.float32) ** block_scale(key_of[0], (SCENARIOS, LINKS), ((0, 4), (1, 8)), -0.2, 0.2)), 0.2, 1.0)
    free_time = draw_free_time(jax.random.fold_in(key_of[9], 71), 0)
    capacity = jnp.clip(jnp.exp(math.log(1.5) - 1.0986123 * jax.random.uniform(key_of[2], (LINKS,), jnp.float32) ** block_scale(key_of[2], (LINKS,), ((0, 8),), -0.2, 0.2)), 0.5, 1.5)
    demand = jnp.clip(0.05 + 0.25 * jax.random.uniform(key_of[3], (SCENARIOS, N_DOM, OD_DEV), jnp.float32) ** block_scale(key_of[3], (SCENARIOS, N_DOM, OD_DEV), ((0, 4), (1, 8)), -0.2, 0.2), 0.05, 0.3)
    path_od = jax.vmap(lambda own: jnp.searchsorted(jnp.cumsum(ragged_sizes(own, OD_DEV, PATHS_DEV, 8, 1)), jnp.arange(PATHS_DEV), side="right"))(jax.random.split(key_of[4], N_DOM)).reshape((N_DOM, PATHS_DEV)).astype(jnp.int32)
    send_blocks = set_ends(jax.random.randint(key_of[5], (N_DOM, N_DOM, CAP), 0, LINK_BLOCKS), jax.random.fold_in(key_of[5], 1), 0, LINK_BLOCKS - 1).astype(jnp.int32)
    send_counts = draw_send_counts(jax.random.fold_in(key_of[9], 71), 0)
    tile_links = set_ends(jax.random.randint(key_of[7], (N_DOM, N_DOM, CAP, HOPS, BLOCK), 0 - BLOCK, BLOCK), jax.random.fold_in(key_of[7], 1), 0 - BLOCK, BLOCK - 1).astype(jnp.int32)
    tile_paths = set_ends(jax.random.randint(key_of[8], (N_DOM, N_DOM, CAP), 0, PATH_BLOCKS), jax.random.fold_in(key_of[8], 1), 0, PATH_BLOCKS - 1).astype(jnp.int32)
    return dict(link_flow=link_flow, free_time=free_time, capacity=capacity, demand=demand, path_od=path_od, send_blocks=send_blocks, send_counts=send_counts, tile_links=tile_links, tile_paths=tile_paths)


dispersion = 2.0


def bpr_times(current, free_time, capacity):
    loading = current / capacity
    square = loading * loading
    return free_time * (1.0 + 0.15 * square * square)


def link_path_incidence(link_rows):
    positions = jnp.arange(link_rows.shape[-1], dtype=jnp.int32)
    return jnp.sum((link_rows[:, :, None, :] == positions[None, None, :, None]).astype(jnp.float32), axis=1)


def logit_split(path_cost, anchor_dest, demands):
    pair_count = demands.shape[1]
    lowest = jnp.full((path_cost.shape[0], pair_count), jnp.inf, path_cost.dtype).at[:, anchor_dest].min(path_cost)
    weight = jnp.exp(-dispersion * (path_cost - lowest[:, anchor_dest]))
    weight_sum = jnp.zeros((path_cost.shape[0], pair_count), path_cost.dtype).at[:, anchor_dest].add(weight)
    return demands[:, anchor_dest] * weight / weight_sum[:, anchor_dest]


def reference(link_flow, free_time, capacity, demand, path_od, send_blocks, send_counts, tile_links, tile_paths):
    scenarios = link_flow.shape[0]
    tile_count = N_DOM * CAP
    slot_ids = jnp.arange(CAP, dtype=jnp.int32)
    live_mask = (slot_ids[None, None, :] < send_counts[:, :, None]).astype(jnp.float32)
    offsets = (jnp.arange(N_DOM, dtype=jnp.int32) * LINK_BLOCKS)[None, :, None]
    global_blocks = (jnp.transpose(send_blocks, (1, 0, 2)) + offsets).astype(jnp.int32).reshape(N_DOM, tile_count)
    live_owner = jnp.transpose(live_mask, (1, 0, 2)).reshape(N_DOM, tile_count)
    demand_owner = jnp.transpose(demand, (1, 0, 2))
    current = link_flow
    path_rows = None
    for iteration in range(ITERS):
        link_times = bpr_times(current, free_time, capacity).reshape(scenarios, N_DOM * LINK_BLOCKS, BLOCK)

        def owner_round(accumulated, payload):
            global_block, tile_live, link_rows, path_block, anchor_dest, demands = payload
            section_travel_times = jnp.take(link_times, global_block, axis=1) * tile_live[None, :, None]
            one_hot_selector = link_path_incidence(link_rows.reshape(tile_count, HOPS, BLOCK))
            partial_link_value = jnp.einsum("cbe,bek->bck", section_travel_times, one_hot_selector, precision=lax.Precision.HIGHEST)
            block_ids = path_block.reshape(tile_count)
            path_cost = jax.ops.segment_sum(partial_link_value, block_ids, num_segments=PATH_BLOCKS)
            path_cost = jnp.transpose(path_cost, (1, 0, 2)).reshape(scenarios, PATH_BLOCKS * BLOCK)
            path_flow = logit_split(path_cost, anchor_dest, demands)
            section_flow = jnp.take(path_flow.reshape(scenarios, PATH_BLOCKS, BLOCK), block_ids, axis=1)
            loaded_link_flow = jnp.einsum("mwa,wya->wmy", section_flow, one_hot_selector, precision=lax.Precision.HIGHEST)
            loaded_link_flow = loaded_link_flow * tile_live[:, None, None]
            return accumulated.at[global_block].add(loaded_link_flow), path_flow

        initial = jnp.zeros((N_DOM * LINK_BLOCKS, scenarios, BLOCK), jnp.float32)
        auxiliary, path_rows = lax.scan(owner_round, initial, (global_blocks, live_owner, tile_links, tile_paths, path_od, demand_owner))
        auxiliary = jnp.transpose(auxiliary, (1, 0, 2)).reshape(scenarios, N_DOM * LINK_BLOCKS * BLOCK)
        current = current + (auxiliary - current) / (iteration + 2.0)
    path_flow = jnp.transpose(path_rows, (1, 0, 2)).reshape(scenarios, N_DOM * PATH_BLOCKS * BLOCK)
    mean_time = jnp.sum(bpr_times(current, free_time, capacity), axis=0) / scenarios
    return current, path_flow, mean_time
```

```python
import functools

import jax
import jax.numpy as jnp
from jax import lax
from jax.experimental import pallas as pl
from jax.experimental.pallas import tpu as pltpu
from jax.sharding import PartitionSpec as P

ITERS = 2
MAX_RUN = 8
dispersion = 2.0
MESH = pl.DeviceIdType.MESH


def split3(value):
    high = value.astype(jnp.bfloat16)
    rest = value - high.astype(jnp.float32)
    mid = rest.astype(jnp.bfloat16)
    low = (rest - mid.astype(jnp.float32)).astype(jnp.bfloat16)
    return jnp.concatenate([high, mid, low], axis=0)


def join3(product):
    rows = product.shape[0] // 3
    return (product[2 * rows :] + product[rows : 2 * rows]) + product[:rows]


def offset(i, n):
    return n // 2 + (2 * (i % 2) - 1) * ((i + 1) // 2)


def kernel(
    n,
    m,
    x_ref,
    free_ref,
    cap_ref,
    demand_ref,
    od_ref,
    block_ref,
    count_ref,
    links_ref,
    tile_path_ref,
    load_ref,
    flow_ref,
    mean_ref,
    times,
    fsend,
    frecv,
    rsend,
    rrecv,
    incidence,
    factor,
    pick,
    masks,
    pair_demand,
    flow3,
    ens_buf,
    fs_sem,
    fr_sem,
    rs_sem,
    rr_sem,
    es_sem,
    er_sem,
):
    me = lax.axis_index("dom")
    ens = lax.axis_index("ens")
    scen = x_ref.shape[0]
    width = links_ref.shape[-1]
    hops = links_ref.shape[3]
    slots = links_ref.shape[2]
    link_blocks = x_ref.shape[1] // width
    paths = od_ref.shape[1]
    path_blocks = paths // width
    pairs = demand_ref.shape[1]

    barrier = pltpu.get_barrier_semaphore()
    for i in range(n - 1):
        pl.semaphore_signal(
            barrier, inc=1, device_id={"dom": lax.rem(me + 1 + i, n)}, device_id_type=MESH
        )
    for i in range(m - 1):
        pl.semaphore_signal(
            barrier, inc=1, device_id={"ens": lax.rem(ens + 1 + i, m)}, device_id_type=MESH
        )

    def forward_copy(j, src, dst, peer):
        return pltpu.make_async_remote_copy(
            src_ref=fsend.at[j, src],
            dst_ref=frecv.at[j, dst],
            send_sem=fs_sem.at[j, src],
            recv_sem=fr_sem.at[j, dst],
            device_id={"dom": peer},
            device_id_type=MESH,
        )

    def return_copy(j, src, dst, peer):
        return pltpu.make_async_remote_copy(
            src_ref=rsend.at[j, src],
            dst_ref=rrecv.at[j, dst],
            send_sem=rs_sem.at[j, src],
            recv_sem=rr_sem.at[j, dst],
            device_id={"dom": peer},
            device_id_type=MESH,
        )

    def ens_copy(dst, peer, slot):
        return pltpu.make_async_remote_copy(
            src_ref=ens_buf.at[ens],
            dst_ref=ens_buf.at[dst],
            send_sem=es_sem.at[slot],
            recv_sem=er_sem.at[dst],
            device_id={"ens": peer},
            device_id_type=MESH,
        )

    def bpr(g, value):
        loading = value / cap_ref[g : g + 1, :]
        square = loading * loading
        return free_ref[g : g + 1, :] * (1.0 + 0.15 * square * square)

    def tile_times(r, k):
        live = jnp.where(k < count_ref[0, r], 1.0, 0.0)
        return times[block_ref[0, k, r]] * live

    def send_times(j):
        def body(i, carry):
            r = lax.rem(me + offset(i, n), n)
            for k in range(slots):
                fsend[j, r, k] = tile_times(r, k)
            forward_copy(j, r, me, r).start()
            return carry

        lax.fori_loop(0, n - 1, body, 0)
        for k in range(slots):
            frecv[j, me, k] = tile_times(me, k)

    def fold_cost(j, s, acc):
        acc = list(acc)
        for k in range(slots):
            part = join3(
                jnp.dot(
                    split3(frecv[j, s, k]),
                    incidence[s * slots + k],
                    preferred_element_type=jnp.float32,
                )
            )
            for b in range(path_blocks):
                acc[b] = acc[b] + pick[s * slots + k, b : b + 1, :] * part
        return tuple(acc)

    def gather_cost(j):
        zero = jnp.zeros((scen, width), jnp.float32)
        acc = fold_cost(j, me, (zero,) * path_blocks)

        def body(i, acc):
            s = lax.rem(me - offset(n - 2 - i, n) + n, n)
            forward_copy(j, s, s, s).wait_recv()
            return fold_cost(j, s, acc)

        acc = lax.fori_loop(0, n - 1, body, acc)
        return jnp.concatenate(acc, axis=1)

    shifts = []
    step = 1
    while step < MAX_RUN:
        shifts.append(step)
        step *= 2

    def logit(cost):
        before, after = cost, cost
        for i, d in enumerate(shifts):
            before = jnp.where(
                masks[2 * i] > 0.0, jnp.minimum(before, pltpu.roll(before, d, 1)), before
            )
            after = jnp.where(
                masks[2 * i + 1] > 0.0, jnp.minimum(after, pltpu.roll(after, paths - d, 1)), after
            )
        weight = jnp.exp(-dispersion * (cost - jnp.minimum(before, after)))
        before, after = weight, weight
        for i, d in enumerate(shifts):
            before = before + masks[2 * i] * pltpu.roll(before, d, 1)
            after = after + masks[2 * i + 1] * pltpu.roll(after, paths - d, 1)
        return pair_demand[...] * weight / (before + (after - weight))

    def tile_flow(s, k):
        return join3(
            lax.dot_general(
                flow3[tile_path_ref[0, k, s]],
                incidence[s * slots + k],
                (((1,), (1,)), ((), ())),
                preferred_element_type=jnp.float32,
            )
        )

    def send_flows(j):
        def body(i, carry):
            s = lax.rem(me + offset(i, n), n)
            for k in range(slots):
                rsend[j, s, k] = tile_flow(s, k)
            return_copy(j, s, me, s).start()
            return carry

        lax.fori_loop(0, n - 1, body, 0)
        for k in range(slots):
            rrecv[j, me, k] = tile_flow(me, k)

    def fold_load(j, r, acc):
        acc = list(acc)
        for k in range(slots):
            tile = rrecv[j, r, k]
            for g in range(link_blocks):
                acc[g] = acc[g] + factor[r * slots + k, g : g + 1, :] * tile
        return tuple(acc)

    def gather_load(j):
        zero = jnp.zeros((scen, width), jnp.float32)
        acc = fold_load(j, me, (zero,) * link_blocks)

        def body(i, acc):
            r = lax.rem(me - offset(n - 2 - i, n) + n, n)
            return_copy(j, r, r, r).wait_recv()
            return fold_load(j, r, acc)

        return lax.fori_loop(0, n - 1, body, acc)

    def columns(g):
        return slice(g * width, (g + 1) * width)

    for g in range(link_blocks):
        times[g] = bpr(g, x_ref[:, columns(g)])
    pl.semaphore_wait(barrier, n + m - 2)
    send_times(0)

    rows = lax.broadcasted_iota(jnp.int32, (width, width), 0)
    link_ids = lax.broadcasted_iota(jnp.int32, (link_blocks, width), 0)
    path_ids = lax.broadcasted_iota(jnp.int32, (path_blocks, width), 0)

    def tables(s, carry):
        for k in range(slots):
            t = s * slots + k
            links = links_ref[0, s, k]
            count = jnp.zeros((width, width), jnp.float32)
            for h in range(hops):
                count = count + jnp.where(links[h : h + 1, :] == rows, 1.0, 0.0)
            incidence[t] = count.astype(jnp.bfloat16)
            pick[t] = jnp.where(path_ids == tile_path_ref[0, k, s], 1.0, 0.0)
            live = jnp.where(k < count_ref[0, s], 1.0, 0.0)
            factor[t] = jnp.where(link_ids == block_ref[0, k, s], 1.0, 0.0) * live
        return carry

    lax.fori_loop(0, n, tables, 0)
    od = jnp.broadcast_to(od_ref[...], (scen, paths))
    for i, d in enumerate(shifts):
        masks[2 * i] = jnp.where(pltpu.roll(od, d, 1) == od, 1.0, 0.0)
        masks[2 * i + 1] = jnp.where(pltpu.roll(od, paths - d, 1) == od, 1.0, 0.0)
    demand3 = split3(demand_ref[...])
    pair_ids = lax.broadcasted_iota(jnp.int32, (pairs, width), 0)
    for b in range(path_blocks):
        chosen = jnp.where(od_ref[:, columns(b)] == pair_ids, 1.0, 0.0).astype(jnp.bfloat16)
        pair_demand[:, columns(b)] = join3(
            jnp.dot(demand3, chosen, preferred_element_type=jnp.float32)
        )

    current_ref = x_ref
    for j in range(ITERS):
        if j > 0:
            send_times(j)
        flow = logit(gather_cost(j))
        if j == ITERS - 1:
            flow_ref[...] = flow
        for b in range(path_blocks):
            flow3[b] = split3(flow[:, columns(b)])
        send_flows(j)
        loads = gather_load(j)
        for g in range(link_blocks):
            current = current_ref[:, columns(g)]
            current = current + (loads[g] - current) / (j + 2.0)
            load_ref[:, columns(g)] = current
            link_time = bpr(g, current)
            if j < ITERS - 1:
                times[g] = link_time
            else:
                ens_buf[ens, g : g + 1, :] = jnp.sum(link_time, axis=0, keepdims=True)
        current_ref = load_ref

    for i in range(1, m):
        ens_copy(ens, lax.rem(ens + i, m), i).start()
    for j in range(ITERS):

        def drain(i, carry):
            r = lax.rem(me + offset(i, n), n)
            forward_copy(j, r, me, r).wait_send()
            return_copy(j, r, me, r).wait_send()
            return carry

        lax.fori_loop(0, n - 1, drain, 0)
    for i in range(1, m):
        peer = lax.rem(ens + m - i, m)
        ens_copy(peer, peer, i).wait_recv()
    total = ens_buf[0]
    for i in range(1, m):
        total = total + ens_buf[i]
    mean_ref[...] = total / (scen * m)
    for i in range(1, m):
        ens_copy(ens, lax.rem(ens + i, m), i).wait_send()


def local(
    n,
    m,
    link_flow,
    free_time,
    capacity,
    demand,
    path_od,
    send_blocks,
    send_counts,
    tile_links,
    tile_paths,
):
    scen, links = link_flow.shape
    width = tile_links.shape[-1]
    slots = tile_links.shape[2]
    tiles = n * slots
    link_blocks = links // width
    paths = path_od.shape[1]
    path_blocks = paths // width
    pairs = demand.shape[2]
    f32 = jnp.float32
    mask_count = 2 * max(1, (MAX_RUN - 1).bit_length())
    exchange = pltpu.VMEM((ITERS, n, slots, scen, width), f32)
    vmem = pl.BlockSpec(memory_space=pltpu.VMEM)
    smem = pl.BlockSpec(memory_space=pltpu.SMEM)
    load, flow, mean = pl.pallas_call(
        functools.partial(kernel, n, m),
        out_shape=(
            jax.ShapeDtypeStruct((scen, links), f32),
            jax.ShapeDtypeStruct((scen, paths), f32),
            jax.ShapeDtypeStruct((link_blocks, width), f32),
        ),
        in_specs=[vmem, vmem, vmem, vmem, vmem, smem, smem, vmem, smem],
        out_specs=(vmem, vmem, vmem),
        scratch_shapes=[
            pltpu.VMEM((link_blocks, scen, width), f32),
            exchange,
            exchange,
            exchange,
            exchange,
            pltpu.VMEM((tiles, width, width), jnp.bfloat16),
            pltpu.VMEM((tiles, link_blocks, width), f32),
            pltpu.VMEM((tiles, path_blocks, width), f32),
            pltpu.VMEM((mask_count, scen, paths), f32),
            pltpu.VMEM((scen, paths), f32),
            pltpu.VMEM((path_blocks, 3 * scen, width), jnp.bfloat16),
            pltpu.VMEM((m, link_blocks, width), f32),
            pltpu.SemaphoreType.DMA((ITERS, n)),
            pltpu.SemaphoreType.DMA((ITERS, n)),
            pltpu.SemaphoreType.DMA((ITERS, n)),
            pltpu.SemaphoreType.DMA((ITERS, n)),
            pltpu.SemaphoreType.DMA((m,)),
            pltpu.SemaphoreType.DMA((m,)),
        ],
        compiler_params=pltpu.CompilerParams(
            collective_id=0, has_side_effects=True, vmem_limit_bytes=56 * 1024 * 1024
        ),
        name="equilibrium",
    )(
        link_flow,
        free_time.reshape(link_blocks, width),
        capacity.reshape(link_blocks, width),
        demand.reshape(scen, pairs),
        path_od,
        jnp.swapaxes(send_blocks, 1, 2),
        send_counts,
        tile_links,
        jnp.swapaxes(tile_paths, 1, 2),
    )
    return load, flow, mean.reshape(links)


def solution(mesh):
    in_specs = (
        P("ens", "dom"),
        P("dom"),
        P("dom"),
        P("ens", "dom", None),
        P("dom", None),
        P("dom", None, None),
        P("dom", None),
        P("dom", None, None, None, None),
        P("dom", None, None),
    )
    out_specs = (P("ens", "dom"), P("ens", "dom"), P("dom"))
    body = functools.partial(local, mesh.shape["dom"], mesh.shape["ens"])
    return jax.shard_map(body, mesh=mesh, in_specs=in_specs, out_specs=out_specs, check_vma=False)
```

```python
import functools

import jax
import jax.numpy as jnp
from jax import lax
from jax.experimental import pallas as pl
from jax.experimental.pallas import tpu as pltpu
from jax.sharding import PartitionSpec as P

ITERS = 2
MAX_RUN = 8
dispersion = 2.0
MESH = pl.DeviceIdType.MESH


def split3(value):
    high = value.astype(jnp.bfloat16).astype(jnp.float32)
    rest = value - high
    mid = rest.astype(jnp.bfloat16).astype(jnp.float32)
    return jnp.concatenate([high, mid, rest - mid], axis=0).astype(jnp.bfloat16)


def join3(product):
    rows = product.shape[0] // 3
    return (product[2 * rows :] + product[rows : 2 * rows]) + product[:rows]


def partner(me, i, n):
    step = n - 1 - i
    if n & (n - 1):
        return lax.rem(me + step, n)
    other = 0
    bit = 1
    while bit < n:
        other = other + lax.rem(me // bit + step // bit, 2) * bit
        bit *= 2
    return other


def kernel(
    n,
    m,
    streams,
    x_hbm,
    free_hbm,
    cap_hbm,
    demand_hbm,
    od_hbm,
    block_hbm,
    count_hbm,
    links_hbm,
    tile_path_hbm,
    load_hbm,
    flow_hbm,
    mean_hbm,
    x_ref,
    free_ref,
    cap_ref,
    demand_ref,
    od_ref,
    block_ref,
    count_ref,
    links_ref,
    tile_path_ref,
    load_ref,
    flow_ref,
    mean_ref,
    in_sem,
    out_sem,
    times,
    fsend,
    frecv,
    rsend,
    rrecv,
    incidence,
    factor,
    pick,
    masks,
    pair_demand,
    flow3,
    ens_buf,
    fs_sem,
    fr_sem,
    rs_sem,
    rr_sem,
    es_sem,
    er_sem,
):
    me = lax.axis_index("dom")
    ens = lax.axis_index("ens")
    scen = x_ref.shape[0] // streams
    width = links_ref.shape[-1]
    hops = links_ref.shape[3]
    slots = links_ref.shape[2]
    link_blocks = x_ref.shape[1] // width
    paths = od_ref.shape[1]
    path_blocks = paths // width
    pairs = demand_ref.shape[2]

    barrier = pltpu.get_barrier_semaphore()
    for i in range(n - 1):
        pl.semaphore_signal(
            barrier, inc=1, device_id={"dom": lax.rem(me + 1 + i, n)}, device_id_type=MESH
        )
    for i in range(m - 1):
        pl.semaphore_signal(
            barrier, inc=1, device_id={"ens": lax.rem(ens + 1 + i, m)}, device_id_type=MESH
        )

    staged = (
        (x_hbm, x_ref),
        (free_hbm, free_ref),
        (cap_hbm, cap_ref),
        (block_hbm, block_ref),
        (count_hbm, count_ref),
        (links_hbm, links_ref),
        (tile_path_hbm, tile_path_ref),
        (od_hbm, od_ref),
        (demand_hbm, demand_ref),
    )
    staging = [
        pltpu.make_async_copy(src, dst, in_sem.at[i]) for i, (src, dst) in enumerate(staged)
    ]
    for copy in staging:
        copy.start()

    def forward_copy(j, src, dst, peer):
        return pltpu.make_async_remote_copy(
            src_ref=fsend.at[j, src],
            dst_ref=frecv.at[j, dst],
            send_sem=fs_sem.at[j, src],
            recv_sem=fr_sem.at[j, dst],
            device_id={"dom": peer},
            device_id_type=MESH,
        )

    def return_copy(j, src, dst, peer):
        return pltpu.make_async_remote_copy(
            src_ref=rsend.at[j, src],
            dst_ref=rrecv.at[j, dst],
            send_sem=rs_sem.at[j, src],
            recv_sem=rr_sem.at[j, dst],
            device_id={"dom": peer},
            device_id_type=MESH,
        )

    def ens_copy(dst, peer, slot):
        return pltpu.make_async_remote_copy(
            src_ref=ens_buf.at[ens],
            dst_ref=ens_buf.at[dst],
            send_sem=es_sem.at[slot],
            recv_sem=er_sem.at[dst],
            device_id={"ens": peer},
            device_id_type=MESH,
        )

    def bpr(g, value):
        loading = value / cap_ref[g : g + 1, :]
        square = loading * loading
        return free_ref[g : g + 1, :] * (1.0 + 0.15 * square * square)

    def tile_times(h, r, k):
        live = jnp.where(k < count_ref[0, r], 1.0, 0.0)
        return times[h * link_blocks + block_ref[0, k, r]] * live

    def send_times(h, j):
        def body(i, carry):
            r = partner(me, i, n)
            for k in range(slots):
                fsend[j, r, k] = tile_times(h, r, k)
            forward_copy(j, r, me, r).start()
            return carry

        lax.fori_loop(0, n - 1, body, 0, unroll=n <= 8)
        for k in range(slots):
            frecv[j, me, k] = tile_times(h, me, k)

    def fold_cost(j, s, acc):
        acc = list(acc)
        for k in range(slots):
            part = join3(
                jnp.dot(
                    split3(frecv[j, s, k]),
                    incidence[s * slots + k],
                    preferred_element_type=jnp.float32,
                )
            )
            for b in range(path_blocks):
                acc[b] = acc[b] + pick[s * slots + k, b : b + 1, :] * part
        return tuple(acc)

    def gather_cost(j):
        zero = jnp.zeros((scen, width), jnp.float32)
        acc = fold_cost(j, me, (zero,) * path_blocks)

        def body(i, acc):
            s = partner(me, i, n)
            forward_copy(j, s, s, s).wait_recv()
            return fold_cost(j, s, acc)

        acc = lax.fori_loop(0, n - 1, body, acc, unroll=n <= 8)
        return jnp.concatenate(acc, axis=1)

    shifts = []
    step = 1
    while step < MAX_RUN:
        shifts.append(step)
        step *= 2

    def rows_of(h):
        return slice(h * scen, (h + 1) * scen)

    def logit(h, cost):
        before, after = cost, cost
        for i, d in enumerate(shifts):
            before = jnp.where(
                masks[2 * i] > 0.0, jnp.minimum(before, pltpu.roll(before, d, 1)), before
            )
            after = jnp.where(
                masks[2 * i + 1] > 0.0, jnp.minimum(after, pltpu.roll(after, paths - d, 1)), after
            )
        weight = jnp.exp(-dispersion * (cost - jnp.minimum(before, after)))
        before, after = weight, weight
        for i, d in enumerate(shifts):
            before = before + masks[2 * i] * pltpu.roll(before, d, 1)
            after = after + masks[2 * i + 1] * pltpu.roll(after, paths - d, 1)
        return pair_demand[rows_of(h), :] * weight / (before + (after - weight))

    def tile_flow(h, s, k):
        return join3(
            lax.dot_general(
                flow3[h * path_blocks + tile_path_ref[0, k, s]],
                incidence[s * slots + k],
                (((1,), (1,)), ((), ())),
                preferred_element_type=jnp.float32,
            )
        )

    def send_flows(h, j):
        def body(i, carry):
            s = partner(me, i, n)
            for k in range(slots):
                rsend[j, s, k] = tile_flow(h, s, k)
            return_copy(j, s, me, s).start()
            return carry

        lax.fori_loop(0, n - 1, body, 0, unroll=n <= 8)
        for k in range(slots):
            rrecv[j, me, k] = tile_flow(h, me, k)

    def fold_load(j, r, acc):
        acc = list(acc)
        for k in range(slots):
            tile = rrecv[j, r, k]
            for g in range(link_blocks):
                acc[g] = acc[g] + factor[r * slots + k, g : g + 1, :] * tile
        return tuple(acc)

    def gather_load(j):
        zero = jnp.zeros((scen, width), jnp.float32)
        acc = fold_load(j, me, (zero,) * link_blocks)

        def body(i, acc):
            r = partner(me, i, n)
            return_copy(j, r, r, r).wait_recv()
            return fold_load(j, r, acc)

        return lax.fori_loop(0, n - 1, body, acc, unroll=n <= 8)

    def columns(g):
        return slice(g * width, (g + 1) * width)

    for copy in staging[:5]:
        copy.wait()
    for h in range(streams):
        for g in range(link_blocks):
            times[h * link_blocks + g] = bpr(g, x_ref[rows_of(h), columns(g)])
    pl.semaphore_wait(barrier, n + m - 2)
    for h in range(streams):
        send_times(h, h)
    for copy in staging[5:]:
        copy.wait()

    rows = lax.broadcasted_iota(jnp.int32, (width, width), 0)
    link_ids = lax.broadcasted_iota(jnp.int32, (link_blocks, width), 0)
    path_ids = lax.broadcasted_iota(jnp.int32, (path_blocks, width), 0)

    def tables(s, carry):
        for k in range(slots):
            t = s * slots + k
            links = links_ref[0, s, k]
            count = jnp.zeros((width, width), jnp.float32)
            for h in range(hops):
                count = count + jnp.where(links[h : h + 1, :] == rows, 1.0, 0.0)
            incidence[t] = count.astype(jnp.bfloat16)
            pick[t] = jnp.where(path_ids == tile_path_ref[0, k, s], 1.0, 0.0)
            live = jnp.where(k < count_ref[0, s], 1.0, 0.0)
            factor[t] = jnp.where(link_ids == block_ref[0, k, s], 1.0, 0.0) * live
        return carry

    lax.fori_loop(0, n, tables, 0)
    od = jnp.broadcast_to(od_ref[...], (scen, paths))
    for i, d in enumerate(shifts):
        masks[2 * i] = jnp.where(pltpu.roll(od, d, 1) == od, 1.0, 0.0)
        masks[2 * i + 1] = jnp.where(pltpu.roll(od, paths - d, 1) == od, 1.0, 0.0)
    demand3 = split3(demand_ref[:, 0, :])
    pair_ids = lax.broadcasted_iota(jnp.int32, (pairs, width), 0)
    for b in range(path_blocks):
        chosen = jnp.where(od_ref[:, columns(b)] == pair_ids, 1.0, 0.0).astype(jnp.bfloat16)
        pair_demand[:, columns(b)] = join3(
            jnp.dot(demand3, chosen, preferred_element_type=jnp.float32)
        )

    flow_copy = pltpu.make_async_copy(flow_ref, flow_hbm, out_sem.at[0])
    load_copy = pltpu.make_async_copy(load_ref, load_hbm, out_sem.at[1])
    mean_copy = pltpu.make_async_copy(mean_ref, mean_hbm, out_sem.at[2])
    current_ref = x_ref
    for j in range(ITERS):
        last = j == ITERS - 1
        for h in range(streams):
            phase = j * streams + h
            flow = logit(h, gather_cost(phase))
            if last:
                flow_ref[rows_of(h), :] = flow
            for b in range(path_blocks):
                flow3[h * path_blocks + b] = split3(flow[:, columns(b)])
            send_flows(h, phase)
        if last:
            flow_copy.start()
        for h in range(streams):
            phase = j * streams + h
            loads = gather_load(phase)
            for g in range(link_blocks):
                current = current_ref[rows_of(h), columns(g)]
                current = current + (loads[g] - current) / (j + 2.0)
                load_ref[rows_of(h), columns(g)] = current
                link_time = bpr(g, current)
                if not last:
                    times[h * link_blocks + g] = link_time
                else:
                    summed = jnp.sum(link_time, axis=0, keepdims=True)
                    if h > 0:
                        summed = summed + ens_buf[ens, g : g + 1, :]
                    ens_buf[ens, g : g + 1, :] = summed
            if not last:
                send_times(h, phase + streams)
        current_ref = load_ref

    for i in range(1, m):
        ens_copy(ens, lax.rem(ens + i, m), i).start()
    load_copy.start()

    def drain(i, carry):
        r = partner(me, i, n)
        for phase in range(ITERS * streams):
            forward_copy(phase, r, me, r).wait_send()
            return_copy(phase, r, me, r).wait_send()
        return carry

    lax.fori_loop(0, n - 1, drain, 0)
    for i in range(1, m):
        peer = lax.rem(ens + m - i, m)
        ens_copy(peer, peer, i).wait_recv()
    total = ens_buf[0]
    for i in range(1, m):
        total = total + ens_buf[i]
    mean_ref[...] = total / (x_ref.shape[0] * m)
    mean_copy.start()
    for i in range(1, m):
        ens_copy(ens, lax.rem(ens + i, m), i).wait_send()
    flow_copy.wait()
    load_copy.wait()
    mean_copy.wait()


def finish(a, b, c, oa, ob, oc, va, vb, vc, in_sem, out_sem):
    triples = ((a, va, oa), (b, vb, ob), (c, vc, oc))
    loads = [pltpu.make_async_copy(s, v, in_sem.at[i]) for i, (s, v, _) in enumerate(triples)]
    stores = [pltpu.make_async_copy(v, o, out_sem.at[i]) for i, (_, v, o) in enumerate(triples)]
    for copy in loads:
        copy.start()
    for load, store in zip(loads, stores):
        load.wait()
        store.start()
    for copy in stores:
        copy.wait()


def local(
    n,
    m,
    link_flow,
    free_time,
    capacity,
    demand,
    path_od,
    send_blocks,
    send_counts,
    tile_links,
    tile_paths,
):
    scen, links = link_flow.shape
    width = tile_links.shape[-1]
    slots = tile_links.shape[2]
    tiles = n * slots
    link_blocks = links // width
    paths = path_od.shape[1]
    path_blocks = paths // width
    pairs = demand.shape[2]
    f32 = jnp.float32
    mask_count = 2 * max(1, (MAX_RUN - 1).bit_length())
    streams = 1
    phases = ITERS * streams
    part = scen // streams
    exchange = pltpu.VMEM((phases, n, slots, part, width), f32)
    stay = pl.BlockSpec(memory_space=pl.ANY)
    i32 = jnp.int32
    load, flow, mean = pl.pallas_call(
        functools.partial(kernel, n, m, streams),
        out_shape=(
            jax.ShapeDtypeStruct((scen, links), f32),
            jax.ShapeDtypeStruct((scen, paths), f32),
            jax.ShapeDtypeStruct((link_blocks, width), f32),
        ),
        in_specs=[stay] * 9,
        out_specs=(stay, stay, stay),
        scratch_shapes=[
            pltpu.VMEM((scen, links), f32),
            pltpu.VMEM((link_blocks, width), f32),
            pltpu.VMEM((link_blocks, width), f32),
            pltpu.VMEM((scen, 1, pairs), f32),
            pltpu.VMEM((1, paths), i32),
            pltpu.SMEM((1, slots, n), i32),
            pltpu.SMEM((1, n), i32),
            pltpu.VMEM(tile_links.shape, i32),
            pltpu.SMEM((1, slots, n), i32),
            pltpu.VMEM((scen, links), f32),
            pltpu.VMEM((scen, paths), f32),
            pltpu.VMEM((link_blocks, width), f32),
            pltpu.SemaphoreType.DMA((9,)),
            pltpu.SemaphoreType.DMA((3,)),
            pltpu.VMEM((streams * link_blocks, part, width), f32),
            exchange,
            exchange,
            exchange,
            exchange,
            pltpu.VMEM((tiles, width, width), jnp.bfloat16),
            pltpu.VMEM((tiles, link_blocks, width), f32),
            pltpu.VMEM((tiles, path_blocks, width), f32),
            pltpu.VMEM((mask_count, part, paths), f32),
            pltpu.VMEM((scen, paths), f32),
            pltpu.VMEM((streams * path_blocks, 3 * part, width), jnp.bfloat16),
            pltpu.VMEM((m, link_blocks, width), f32),
            pltpu.SemaphoreType.DMA((phases, n)),
            pltpu.SemaphoreType.DMA((phases, n)),
            pltpu.SemaphoreType.DMA((phases, n)),
            pltpu.SemaphoreType.DMA((phases, n)),
            pltpu.SemaphoreType.DMA((m,)),
            pltpu.SemaphoreType.DMA((m,)),
        ],
        compiler_params=pltpu.CompilerParams(
            collective_id=0, has_side_effects=True, vmem_limit_bytes=56 * 1024 * 1024
        ),
        name="equilibrium",
    )(
        link_flow,
        free_time.reshape(link_blocks, width),
        capacity.reshape(link_blocks, width),
        demand,
        path_od,
        jnp.swapaxes(send_blocks, 1, 2),
        send_counts,
        tile_links,
        jnp.swapaxes(tile_paths, 1, 2),
    )
    load, flow, mean = pl.pallas_call(
        finish,
        out_shape=(
            jax.ShapeDtypeStruct((scen, links), f32),
            jax.ShapeDtypeStruct((scen, paths), f32),
            jax.ShapeDtypeStruct((link_blocks, width), f32),
        ),
        in_specs=[stay] * 3,
        out_specs=(stay,) * 3,
        scratch_shapes=[
            pltpu.VMEM((scen, links), f32),
            pltpu.VMEM((scen, paths), f32),
            pltpu.VMEM((link_blocks, width), f32),
            pltpu.SemaphoreType.DMA((3,)),
            pltpu.SemaphoreType.DMA((3,)),
        ],
        name="finish",
    )(load, flow, mean)
    return load, flow, mean.reshape(links)


def solution(mesh):
    in_specs = (
        P("ens", "dom"),
        P("dom"),
        P("dom"),
        P("ens", "dom", None),
        P("dom", None),
        P("dom", None, None),
        P("dom", None),
        P("dom", None, None, None, None),
        P("dom", None, None),
    )
    out_specs = (P("ens", "dom"), P("ens", "dom"), P("dom"))
    body = functools.partial(local, mesh.shape["dom"], mesh.shape["ens"])
    return jax.shard_map(body, mesh=mesh, in_specs=in_specs, out_specs=out_specs, check_vma=False)
```
